32 devices in a mesh: groups: 2 (over y), hidden: 4 (over z), cols: 2 (over x), rep: 2 (over core).
Axes of the slice: x: 2, y: 2, z: 4, core: 2. Of those that a mesh axis runs over, the one named last changes fastest.
Arguments:
- inputs: bfloat16 [8192, 28672], P(('groups', 'cols', 'rep'), 'hidden'), parts along dimension 0, may hold values from -6 to 6
- grads: bfloat16 [8192, 8192], P(('groups', 'cols', 'rep'), 'hidden'), parts along dimension 0, may hold values from -1.5 to 1.5
- in_signs: int32 [28672], P('hidden'), may hold values from -1 to 1, as said below
- out_signs: int32 [8192], P('hidden'), may hold values from -1 to 1, as said below
- in_rows: int32 [128], replicated, may hold values from 0 to 28671, as said below
- out_rows: int32 [128], replicated, may hold values from 0 to 8191, as said below
- inv_gram: bfloat16 [16384, 16384], P('hidden', ('cols', 'rep')), may hold values from -0.0625 to 0.0625
Outputs:
- preconditioned: float32 [64, 16384], P('groups', ('cols', 'rep', 'hidden')), parts along dimension 0
The draws below stay inside these ranges and needn't reach their ends.
There are 2 independent parts, one for each index of `groups`. The reference program is written for one: setup_inputs(seed, part) draws one part's arguments, and reference() takes and returns one part's arrays. A program takes and returns all parts, laid end to end along the dimension named above; an argument that names none is the same for every part. Nothing has to cross between parts.
Inputs may be any that keep to these rules, and one draw needn't show every extreme that they name: `in_signs`: each entry is -1 or +1. `out_signs`: each entry is -1 or +1. `in_rows`: distinct. `out_rows`: distinct.
All inputs are finite; a program needn't handle non-finite values.
Results may differ from the reference program's by a relative error of at most 0.0003.
Values sent between devices are 32-bit elements; how exact they have to be, the bound alone decides.
A program may use at most 128 MiB of HBM per device.

```python
import math
import jax
import jax.numpy as jnp
from jax import lax

IN_W = 28672
OUT_W = 8192
HAD = 64
SKETCH = 128
SEQ = 128
GRAM = 16384
TOKENS = 4096


def draw_in_signs(key, part):
    return (2 * jax.random.randint(jax.random.fold_in(key, 101), (IN_W,), 0, 2) - 1).astype(jnp.int32)


def draw_out_signs(key, part):
    return (2 * jax.random.randint(jax.random.fold_in(key, 202), (OUT_W,), 0, 2) - 1).astype(jnp.int32)


def draw_in_rows(key, part):
    return jax.random.permutation(jax.random.fold_in(key, 303), IN_W)[:SKETCH].astype(jnp.int32)


def draw_out_rows(key, part):
    return jax.random.permutation(jax.random.fold_in(key, 404), OUT_W)[:SKETCH].astype(jnp.int32)


def spiked(drawn, own_key, source, target, shards_of, factor):
    def block_of(axis_at):
        return (jnp.arange(drawn.shape[axis_at]) // (drawn.shape[axis_at] // shards_of)).reshape((-1,) + (1,) * (drawn.ndim - 1 - axis_at))

    first = jax.random.permutation(own_key, shards_of)[block_of(target)]
    second = (block_of(target) + shards_of // 2) % shards_of
    return jnp.where((block_of(source) == first) | (block_of(source) == second), factor * drawn, drawn)


def level_of(own_key, dims, split, least, top_value):
    def one(position, blocks):
        steps = jax.random.uniform(jax.random.fold_in(jax.random.fold_in(own_key, 6), position), (blocks,), jnp.float32, least / len(split), top_value / len(split))
        return jnp.repeat(jnp.exp(steps), dims[position] // blocks).reshape((-1,) + (1,) * (len(dims) - position - 1))

    level = one(*split[0])
    for cut in split[1:]:
        level = level * one(*cut)
    return level


def scatter_about(key, dims, scale, reach, shards=(), held_as=jnp.bfloat16):
    values = jax.random.normal(key, dims, jnp.float32) * scale
    if len(shards) > 0:
        values = level_of(key, dims, shards, -0.22, 0.18) * values
    return jnp.clip(values, min=-reach, max=reach).astype(held_as)


def gaussian_with(key, extent, deviation, most, cuts, heavy, kind=jnp.bfloat16):
    array = deviation * jax.random.normal(key, extent, jnp.float32)
    if cuts:
        array = array * level_of(key, extent, cuts, -0.22, 0.18)
    return jnp.clip(spiked(array, jax.random.fold_in(key, 3), *heavy), -most, most).astype(kind)


def setup_inputs(seed: int = 0, part: int = 0) -> dict:
    key_list = jax.random.split(jax.random.key(seed), 8)
    own_keys = jax.random.split(jax.random.fold_in(key_list[7], part), 8)
    return {
        "inputs": scatter_about(own_keys[0], (TOKENS, IN_W), 1.0, 6.0, ((0, 4), (1, 4))),
        "grads": scatter_about(own_keys[1], (TOKENS, OUT_W), 0.25, 1.5, ((0, 4), (1, 4))),
        "in_signs": draw_in_signs(jax.random.fold_in(key_list[7], 71), part),
        "out_signs": draw_out_signs(jax.random.fold_in(key_list[7], 71), part),
        "in_rows": draw_in_rows(jax.random.fold_in(key_list[7], 71), part),
        "out_rows": draw_out_rows(jax.random.fold_in(key_list[7], 71), part),
        "inv_gram": gaussian_with(key_list[6], (GRAM, GRAM), GRAM ** -0.5, 0.0625, ((0, 4), (1, 4)), (0, 1, 4, 2.0)),
    }


def had_sign(left, right):
    both = jnp.bitwise_and(left, right)
    count = jnp.zeros(both.shape, jnp.int32)
    for bit in range(HAD.bit_length() - 1):
        count = count + jnp.bitwise_and(jnp.right_shift(both, bit), 1)
    return (1 - 2 * (count % 2)).astype(jnp.float32)

def sketch(values, signs, rows, width):
    inner = width // HAD
    row_high = (rows // inner).astype(jnp.int32)
    row_low = (rows % inner).astype(jnp.int32)
    cube = values.reshape(values.shape[0], HAD, inner)
    sign_grid = signs.reshape(HAD, inner)
    picked = jnp.take(cube, row_low, axis=2).astype(jnp.float32)
    sources = jnp.arange(HAD, dtype=jnp.int32)
    coef = had_sign(row_high[None, :], sources[:, None]) * jnp.take(sign_grid, row_low, axis=1).astype(jnp.float32) / math.sqrt(HAD)
    return jnp.einsum('thk,hk->tk', picked, coef)

def reference(inputs, grads, in_signs, out_signs, in_rows, out_rows, inv_gram):
    out_sketch = sketch(grads, out_signs, out_rows, OUT_W)
    in_sketch = sketch(inputs, in_signs, in_rows, IN_W)
    count = out_sketch.shape[0] // SEQ
    projected = jnp.einsum('esp,esq->epq', out_sketch.reshape(count, SEQ, SKETCH), in_sketch.reshape(count, SEQ, SKETCH), precision=lax.Precision.HIGHEST)
    projected = projected.reshape(count, GRAM)
    return jnp.dot(projected, inv_gram.astype(jnp.float32), precision=lax.Precision.HIGHEST, preferred_element_type=jnp.float32)
```

```python
import functools
import math

import jax
import jax.numpy as jnp
from jax import lax
from jax.experimental import pallas as pl
from jax.experimental.pallas import tpu as pltpu
from jax.sharding import PartitionSpec as P

IN_W = 28672
OUT_W = 8192
HAD = 64
SKETCH = 128
SEQ = 128
MESH = pl.DeviceIdType.MESH


def had_parity(left, right):
    both = jnp.bitwise_and(left, right)
    for shift in (4, 2, 1):
        both = jnp.bitwise_xor(both, jnp.right_shift(both, shift))
    return jnp.bitwise_and(both, 1)


def split_rows(rows, inner):
    high = jnp.floor((rows.astype(jnp.float32) + 0.5) * (1.0 / inner)).astype(jnp.int32)
    return high, rows - high * inner


def build_matrix(rows_ref, sign_ref, out_ref, shard, width):
    inner = width // HAD
    local_high = sign_ref.shape[0]
    high, low = split_rows(rows_ref[...], inner)
    hit = lax.broadcasted_iota(jnp.int32, (inner, SKETCH), 0) == low
    onehot = jnp.where(hit, 1.0, 0.0)
    picked = jnp.dot(
        sign_ref[...].astype(jnp.bfloat16),
        onehot.astype(jnp.bfloat16),
        preferred_element_type=jnp.float32,
    )
    sources = shard * local_high + lax.broadcasted_iota(jnp.int32, (local_high, SKETCH), 0)
    parity = had_parity(jnp.broadcast_to(high, (local_high, SKETCH)), sources)
    coef = picked * (1 - 2 * parity).astype(jnp.float32) * (1.0 / math.sqrt(HAD))
    for h in range(local_high):
        out_ref[h * inner : (h + 1) * inner, :] = (onehot * coef[h : h + 1, :]).astype(jnp.bfloat16)


def fused_kernel(
    dims,
    x_ref,
    g_ref,
    in_sign_ref,
    out_sign_ref,
    in_rows_ref,
    out_rows_ref,
    gram_ref,
    out_ref,
    x_buf,
    g_buf,
    gram_buf,
    mat_in,
    mat_out,
    part,
    land,
    proj,
    allp,
    wide,
    psum,
    final,
    x_sem,
    g_sem,
    gram_sem,
    send1,
    recv1,
    send2,
    recv2,
    send3,
    recv3,
    send4,
    recv4,
):
    hidden, cols, rep = dims
    me = lax.axis_index("hidden")
    my_col = lax.axis_index("cols")
    my_rep = lax.axis_index("rep")
    tokens = x_buf.shape[1]
    each = tokens // SEQ
    block_p = SKETCH // hidden
    peers = [(c, r) for c in range(cols) for r in range(rep) if (c, r) != (0, 0)]

    def to(k):
        return lax.rem(me + 1 + k, hidden)

    def source(k):
        return lax.rem(me + 2 * hidden - 1 - k, hidden)

    def load_x(k):
        row = pl.multiple_of(to(k) * tokens, tokens)
        return pltpu.make_async_copy(x_ref.at[pl.ds(row, tokens)], x_buf.at[k], x_sem.at[k])

    def load_g(k):
        row = pl.multiple_of(to(k) * tokens, tokens)
        return pltpu.make_async_copy(g_ref.at[pl.ds(row, tokens)], g_buf.at[k], g_sem.at[k])

    gram_parts = gram_sem.shape[0]
    gram_rows = gram_ref.shape[0] // gram_parts

    def load_gram(k):
        where = pl.ds(k * gram_rows, gram_rows)
        return pltpu.make_async_copy(gram_ref.at[where], gram_buf.at[where], gram_sem.at[k])

    for k in range(hidden):
        load_g(k).start()
        load_x(k).start()

    barrier = pltpu.get_barrier_semaphore()
    for k in range(hidden - 1):
        pl.semaphore_signal(barrier, inc=1, device_id={"hidden": to(k)}, device_id_type=MESH)
    for c, r in peers:
        pl.semaphore_signal(
            barrier,
            inc=1,
            device_id={"cols": lax.rem(my_col + c, cols), "rep": lax.rem(my_rep + r, rep)},
            device_id_type=MESH,
        )
    build_matrix(out_rows_ref, out_sign_ref, mat_out, me, OUT_W)
    build_matrix(in_rows_ref, in_sign_ref, mat_in, me, IN_W)
    pl.semaphore_wait(barrier, hidden - 1 + len(peers))

    def send_part(k):
        return pltpu.make_async_remote_copy(
            src_ref=part.at[k],
            dst_ref=land.at[k],
            send_sem=send1.at[k],
            recv_sem=recv1.at[k],
            device_id={"hidden": to(k)},
            device_id_type=MESH,
        )

    def sketch_step(k, carry):
        load_g(k).wait()
        part[k, 0] = jnp.dot(g_buf[k], mat_out[...], preferred_element_type=jnp.float32)
        load_x(k).wait()
        part[k, 1] = jnp.dot(x_buf[k], mat_in[...], preferred_element_type=jnp.float32)

        @pl.when(k < hidden - 1)
        def _():
            send_part(k).start()

        return carry

    lax.fori_loop(0, hidden, sketch_step, 0)
    for k in range(gram_parts):
        load_gram(k).start()
    for k in range(hidden - 1):
        send_part(k).wait_recv()

    for j in range(each):
        at = pl.ds(j * SEQ, SEQ)
        left = part[hidden - 1, 0, at, :]
        right = part[hidden - 1, 1, at, :]
        for k in range(hidden - 1):
            left = left + land[k, 0, at, :]
            right = right + land[k, 1, at, :]
        proj[j] = lax.dot_general(
            left,
            right,
            (((0,), (0,)), ((), ())),
            precision=lax.Precision.HIGHEST,
            preferred_element_type=jnp.float32,
        )

    mine = (my_col * rep + my_rep) * (hidden * each)

    def send_rows(k):
        return pltpu.make_async_remote_copy(
            src_ref=proj.at[:, pl.ds(pl.multiple_of(to(k) * block_p, block_p), block_p), :],
            dst_ref=allp.at[pl.ds(mine + me * each, each)],
            send_sem=send2.at[k],
            recv_sem=recv2.at[k],
            device_id={"hidden": to(k)},
            device_id_type=MESH,
        )

    def arrived_rows(k):
        return pltpu.make_async_remote_copy(
            src_ref=proj.at[:, pl.ds(0, block_p), :],
            dst_ref=allp.at[pl.ds(mine + source(k) * each, each)],
            send_sem=send2.at[k],
            recv_sem=recv2.at[k],
            device_id={"hidden": to(k)},
            device_id_type=MESH,
        )

    for k in range(hidden - 1):
        send_rows(k).start()
    for j in range(each):
        allp[mine + me * each + j] = proj[j, pl.ds(pl.multiple_of(me * block_p, block_p), block_p), :]

    def forward(d, k):
        c, r = peers[d]
        block = allp.at[pl.ds(mine + source(k) * each, each)]
        return pltpu.make_async_remote_copy(
            src_ref=block,
            dst_ref=block,
            send_sem=send3.at[d, k],
            recv_sem=recv3.at[d, k],
            device_id={"cols": lax.rem(my_col + c, cols), "rep": lax.rem(my_rep + r, rep)},
            device_id_type=MESH,
        )

    def forwarded(d, k):
        c, r = peers[d]
        col = lax.rem(my_col + cols - c, cols)
        other = (col * rep + lax.rem(my_rep + rep - r, rep)) * (hidden * each)
        block = allp.at[pl.ds(other + source(k) * each, each)]
        return pltpu.make_async_remote_copy(
            src_ref=block,
            dst_ref=block,
            send_sem=send3.at[d, k],
            recv_sem=recv3.at[d, k],
            device_id={"cols": col},
            device_id_type=MESH,
        )

    for d in range(len(peers)):
        forward(d, hidden - 1).start()
    for k in range(hidden - 1):
        arrived_rows(k).wait_recv()
        for d in range(len(peers)):
            forward(d, k).start()
    for k in range(hidden):
        for d in range(len(peers)):
            forwarded(d, k).wait_recv()

    examples = allp.shape[0]
    for p in range(block_p):
        rows = allp[:, p, :]
        upper = rows.astype(jnp.bfloat16)
        wide[0:examples, p * SKETCH : (p + 1) * SKETCH] = upper
        wide[examples:, p * SKETCH : (p + 1) * SKETCH] = (rows - upper.astype(jnp.float32)).astype(jnp.bfloat16)
    for k in range(gram_parts):
        load_gram(k).wait()

    share = psum.shape[2]
    step = 256
    per = share // step

    def send_sum(k):
        return pltpu.make_async_remote_copy(
            src_ref=psum.at[k],
            dst_ref=final.at[k],
            send_sem=send4.at[k],
            recv_sem=recv4.at[k],
            device_id={"hidden": to(k)},
            device_id_type=MESH,
        )

    def gram_step(n, carry):
        k = n // per
        at = pl.multiple_of(lax.rem(n, per) * step, step)
        column = pl.multiple_of(to(k) * share + at, step)
        both = jnp.dot(wide[...], gram_buf[:, pl.ds(column, step)], preferred_element_type=jnp.float32)
        psum[k, :, pl.ds(at, step)] = both[:examples] + both[examples:]

        @pl.when(jnp.logical_and(lax.rem(n, per) == per - 1, k < hidden - 1))
        def _():
            send_sum(k).start()

        return carry

    lax.fori_loop(0, hidden * per, gram_step, 0)
    total = psum[hidden - 1]
    for k in range(hidden - 1):
        send_sum(k).wait_recv()
        total = total + final[k]
    out_ref[...] = total

    for k in range(hidden - 1):
        send_part(k).wait_send()
        send_rows(k).wait_send()
        send_sum(k).wait_send()
    for k in range(hidden):
        for d in range(len(peers)):
            forward(d, k).wait_send()


def fused(dims, inputs, grads, in_signs, out_signs, in_rows, out_rows, inv_gram):
    hidden, cols, rep = dims
    tokens = inputs.shape[0] // hidden
    count = inputs.shape[0] // SEQ
    each = count // hidden
    block_p = SKETCH // hidden
    examples = count * cols * rep
    share = inv_gram.shape[1] // hidden
    others = cols * rep - 1
    f32 = jnp.float32
    dma = pltpu.SemaphoreType.DMA
    vmem = pl.BlockSpec(memory_space=pltpu.VMEM)
    hbm = pl.BlockSpec(memory_space=pl.ANY)
    gram_parts = 4
    return pl.pallas_call(
        functools.partial(fused_kernel, dims),
        out_shape=jax.ShapeDtypeStruct((examples, share), f32),
        in_specs=[hbm, hbm, vmem, vmem, vmem, vmem, hbm],
        out_specs=vmem,
        scratch_shapes=[
            pltpu.VMEM((hidden, tokens, inputs.shape[1]), jnp.bfloat16),
            pltpu.VMEM((hidden, tokens, grads.shape[1]), jnp.bfloat16),
            pltpu.VMEM(inv_gram.shape, jnp.bfloat16),
            pltpu.VMEM((inputs.shape[1], SKETCH), jnp.bfloat16),
            pltpu.VMEM((grads.shape[1], SKETCH), jnp.bfloat16),
            pltpu.VMEM((hidden, 2, tokens, SKETCH), f32),
            pltpu.VMEM((hidden - 1, 2, tokens, SKETCH), f32),
            pltpu.VMEM((each, SKETCH, SKETCH), f32),
            pltpu.VMEM((examples, block_p, SKETCH), f32),
            pltpu.VMEM((2 * examples, block_p * SKETCH), jnp.bfloat16),
            pltpu.VMEM((hidden, examples, share), f32),
            pltpu.VMEM((hidden - 1, examples, share), f32),
            dma((hidden,)),
            dma((hidden,)),
            dma((gram_parts,)),
            dma((hidden - 1,)),
            dma((hidden - 1,)),
            dma((hidden - 1,)),
            dma((hidden - 1,)),
            dma((others, hidden)),
            dma((others, hidden)),
            dma((hidden - 1,)),
            dma((hidden - 1,)),
        ],
        compiler_params=pltpu.CompilerParams(
            collective_id=0, has_side_effects=True, vmem_limit_bytes=63 << 20
        ),
    )(
        inputs,
        grads,
        in_signs.reshape(inputs.shape[1] // (IN_W // HAD), IN_W // HAD),
        out_signs.reshape(grads.shape[1] // (OUT_W // HAD), OUT_W // HAD),
        in_rows.reshape(1, SKETCH),
        out_rows.reshape(1, SKETCH),
        inv_gram,
    )


def plain_sketch(values, signs, rows, width, shard):
    inner = width // HAD
    local_high = values.shape[1] // inner
    high, low = rows // inner, rows % inner
    feature = jnp.arange(values.shape[1], dtype=jnp.int32)
    sources = shard * local_high + feature // inner
    sign = (1 - 2 * had_parity(high[None, :], sources[:, None])) * signs[:, None]
    hit = (feature % inner)[:, None] == low[None, :]
    matrix = jnp.where(hit, sign.astype(jnp.float32) / math.sqrt(HAD), 0.0)
    return jnp.dot(values, matrix.astype(jnp.bfloat16), preferred_element_type=jnp.float32)


def plain(inputs, grads, in_signs, out_signs, in_rows, out_rows, inv_gram):
    shard = lax.axis_index("hidden")
    out_part = plain_sketch(grads, out_signs, out_rows, OUT_W, shard)
    in_part = plain_sketch(inputs, in_signs, in_rows, IN_W, shard)
    block_p = inv_gram.shape[0] // SKETCH
    count = inputs.shape[0] // SEQ
    out_mine = lax.psum_scatter(out_part, "hidden", scatter_dimension=1, tiled=True)
    in_sketch = lax.psum(in_part, "hidden")
    projected = jnp.einsum(
        "esp,esq->epq",
        out_mine.reshape(count, SEQ, block_p),
        in_sketch.reshape(count, SEQ, SKETCH),
        precision=lax.Precision.HIGHEST,
    )
    projected = projected.reshape(count, block_p * SKETCH)
    partial_out = jnp.dot(
        lax.all_gather(projected, ("cols", "rep"), axis=0, tiled=True),
        inv_gram.astype(jnp.float32),
        precision=lax.Precision.HIGHEST,
        preferred_element_type=jnp.float32,
    )
    return lax.psum_scatter(partial_out, "hidden", scatter_dimension=1, tiled=True)


def solution(mesh):
    dims = tuple(mesh.shape[name] for name in ("hidden", "cols", "rep"))

    def on_device(inputs, *rest):
        if inputs.shape[0] % (dims[0] * SEQ) == 0:
            return fused(dims, inputs, *rest)
        return plain(inputs, *rest)

    return jax.shard_map(
        on_device,
        mesh=mesh,
        in_specs=(
            P(("groups", "cols", "rep"), "hidden"),
            P(("groups", "cols", "rep"), "hidden"),
            P("hidden"),
            P("hidden"),
            P(),
            P(),
            P("hidden", ("cols", "rep")),
        ),
        out_specs=P("groups", ("cols", "rep", "hidden")),
        check_vma=False,
    )
```

```python
import functools
import math

import jax
import jax.numpy as jnp
from jax import lax
from jax.experimental import pallas as pl
from jax.experimental.pallas import tpu as pltpu
from jax.sharding import PartitionSpec as P

IN_W = 28672
OUT_W = 8192
HAD = 64
SKETCH = 128
SEQ = 128
MESH = pl.DeviceIdType.MESH


def had_parity(left, right):
    both = jnp.bitwise_and(left, right)
    for shift in (4, 2, 1):
        both = jnp.bitwise_xor(both, jnp.right_shift(both, shift))
    return jnp.bitwise_and(both, 1)


def split_rows(rows, inner):
    high = jnp.floor((rows.astype(jnp.float32) + 0.5) * (1.0 / inner)).astype(jnp.int32)
    return high, rows - high * inner


def build_matrix(rows_ref, sign_ref, out_ref, shard, width):
    inner = width // HAD
    local_high = sign_ref.shape[0]
    high, low = split_rows(rows_ref[...], inner)
    hit = lax.broadcasted_iota(jnp.int32, (inner, SKETCH), 0) == low
    onehot = jnp.where(hit, 1.0, 0.0)
    picked = jnp.dot(
        sign_ref[...].astype(jnp.bfloat16),
        onehot.astype(jnp.bfloat16),
        preferred_element_type=jnp.float32,
    )
    sources = shard * local_high + lax.broadcasted_iota(jnp.int32, (local_high, SKETCH), 0)
    parity = had_parity(jnp.broadcast_to(high, (local_high, SKETCH)), sources)
    coef = picked * (1 - 2 * parity).astype(jnp.float32) * (1.0 / math.sqrt(HAD))
    for h in range(local_high):
        out_ref[h * inner : (h + 1) * inner, :] = (onehot * coef[h : h + 1, :]).astype(jnp.bfloat16)


def fused_kernel(
    dims,
    x_ref,
    g_ref,
    in_sign_ref,
    out_sign_ref,
    in_rows_ref,
    out_rows_ref,
    gram_ref,
    out_ref,
    x_buf,
    g_buf,
    gram_buf,
    mat_in,
    mat_out,
    part,
    land,
    proj,
    allp,
    wide,
    psum,
    final,
    x_sem,
    g_sem,
    gram_sem,
    send1,
    recv1,
    send2,
    recv2,
    send3,
    recv3,
    send5,
    recv5,
    send4,
    recv4,
):
    hidden, cols, rep = dims
    me = lax.axis_index("hidden")
    my_col = lax.axis_index("cols")
    my_rep = lax.axis_index("rep")
    tokens = x_buf.shape[1]
    each = tokens // SEQ
    block_p = SKETCH // hidden

    def to(k):
        return lax.rem(me + 1 + k, hidden)

    def source(k):
        return lax.rem(me + 2 * hidden - 1 - k, hidden)

    def target(s):
        outer = 1 - lax.rem((me + 1) // 2, 2)
        first = outer * (3 - s) + (1 - outer) * lax.rem(2 + 3 * s, 5)
        return first + (me // 2) * (3 - 2 * first)

    def load_x(k):
        row = pl.multiple_of(target(k) * tokens, tokens)
        return pltpu.make_async_copy(x_ref.at[pl.ds(row, tokens)], x_buf.at[k], x_sem.at[k])

    def load_g(k):
        row = pl.multiple_of(target(k) * tokens, tokens)
        return pltpu.make_async_copy(g_ref.at[pl.ds(row, tokens)], g_buf.at[k], g_sem.at[k])

    gram_parts = gram_sem.shape[0]
    gram_rows = gram_ref.shape[0] // gram_parts

    def load_gram(k):
        where = pl.ds(k * gram_rows, gram_rows)
        return pltpu.make_async_copy(gram_ref.at[where], gram_buf.at[where], gram_sem.at[k])

    for k in range(hidden):
        load_g(k).start()
        load_x(k).start()

    barrier = pltpu.get_barrier_semaphore()
    for k in range(hidden - 1):
        pl.semaphore_signal(barrier, inc=1, device_id={"hidden": to(k)}, device_id_type=MESH)
    for c in range(1, cols):
        pl.semaphore_signal(barrier, inc=1, device_id={"cols": lax.rem(my_col + c, cols)}, device_id_type=MESH)
    for r in range(1, rep):
        pl.semaphore_signal(barrier, inc=1, device_id={"rep": lax.rem(my_rep + r, rep)}, device_id_type=MESH)
    build_matrix(out_rows_ref, out_sign_ref, mat_out, me, OUT_W)
    build_matrix(in_rows_ref, in_sign_ref, mat_in, me, IN_W)
    pl.semaphore_wait(barrier, hidden + cols + rep - 3)

    edge = 1 - lax.rem((me + 1) // 2, 2)
    half = me // 2
    relay = hidden

    def part_copy(s, j):
        passed = edge * (1 - (s + hidden - 1) // hidden)
        slot = me + passed * (relay - me)
        dest = target(s)
        return pltpu.make_async_remote_copy(
            src_ref=part.at[s, j],
            dst_ref=land.at[slot, j],
            send_sem=send1.at[s, j],
            recv_sem=recv1.at[slot, j],
            device_id={"hidden": dest + passed * (1 + half - dest)},
            device_id_type=MESH,
        )

    def part_arrived(slot, j):
        return pltpu.make_async_remote_copy(
            src_ref=part.at[0, j],
            dst_ref=land.at[slot, j],
            send_sem=send1.at[0, j],
            recv_sem=recv1.at[slot, j],
            device_id={"hidden": to(0)},
            device_id_type=MESH,
        )

    def sketch_step(s, carry):
        load_g(s).wait()
        left = jnp.dot(g_buf[s], mat_out[...], preferred_element_type=jnp.float32)
        load_x(s).wait()
        right = jnp.dot(x_buf[s], mat_in[...], preferred_element_type=jnp.float32)
        for j in range(each):
            part[s, j, 0] = left[j * SEQ : (j + 1) * SEQ]
            part[s, j, 1] = right[j * SEQ : (j + 1) * SEQ]

        @pl.when(s < hidden - 2 + edge)
        def _():
            part_copy(s, 0).start()

        return carry

    lax.fori_loop(0, hidden, sketch_step, 0)
    for j in range(1, each):
        for s in range(hidden - 2):
            part_copy(s, j).start()

        @pl.when(edge == 1)
        def _():
            part_copy(hidden - 2, j).start()

    for k in range(gram_parts):
        load_gram(k).start()

    @pl.when(edge == 0)
    def _():
        for j in range(each):
            part_arrived(relay, j).wait_recv()
            part[hidden - 2, j] = part[hidden - 2, j] + land[relay, j]
            part_copy(hidden - 2, j).start()

    def project(j):
        part_arrived(edge, j).wait_recv()
        part_arrived(hidden - 1 - edge, j).wait_recv()
        part[hidden - 1, j] = part[hidden - 1, j] + land[edge, j] + land[hidden - 1 - edge, j]

        @pl.when(edge == 0)
        def _():
            part_arrived(hidden - 1 - me, j).wait_recv()
            part[hidden - 1, j] = part[hidden - 1, j] + land[hidden - 1 - me, j]

        proj[j] = lax.dot_general(
            part[hidden - 1, j, 0],
            part[hidden - 1, j, 1],
            (((0,), (0,)), ((), ())),
            precision=lax.Precision.HIGHEST,
            preferred_element_type=jnp.float32,
        )

    def place(col, r, z, j):
        return ((col * rep + r) * hidden + z) * each + j

    def rows_copy(k, j, z):
        return pltpu.make_async_remote_copy(
            src_ref=proj.at[j, pl.ds(pl.multiple_of(to(k) * block_p, block_p), block_p), :],
            dst_ref=allp.at[place(my_col, my_rep, z, j)],
            send_sem=send2.at[k, j],
            recv_sem=recv2.at[k, j],
            device_id={"hidden": to(k)},
            device_id_type=MESH,
        )

    def col_copy(d, k, j, col):
        block = allp.at[place(col, my_rep, source(k), j)]
        return pltpu.make_async_remote_copy(
            src_ref=block,
            dst_ref=block,
            send_sem=send3.at[d - 1, k, j],
            recv_sem=recv3.at[d - 1, k, j],
            device_id={"cols": lax.rem(my_col + d, cols)},
            device_id_type=MESH,
        )

    def rep_copy(e, d, k, j, r):
        block = allp.at[place(lax.rem(my_col + cols - d, cols), r, source(k), j)]
        return pltpu.make_async_remote_copy(
            src_ref=block,
            dst_ref=block,
            send_sem=send5.at[e - 1, d, k, j],
            recv_sem=recv5.at[e - 1, d, k, j],
            device_id={"rep": lax.rem(my_rep + e, rep)},
            device_id_type=MESH,
        )

    def spread(k, j):
        for d in range(1, cols):
            col_copy(d, k, j, my_col).start()
        for e in range(1, rep):
            rep_copy(e, 0, k, j, my_rep).start()

    def send_rows(j):
        project(j)
        for k in range(hidden - 1):
            rows_copy(k, j, me).start()
        allp[place(my_col, my_rep, me, j)] = proj[j, pl.ds(pl.multiple_of(me * block_p, block_p), block_p), :]
        spread(hidden - 1, j)

    def pass_rows(j):
        for k in range(hidden - 1):
            rows_copy(k, j, source(k)).wait_recv()
            spread(k, j)

    def pass_cols(j):
        for d in range(1, cols):
            for k in [hidden - 1] + list(range(hidden - 1)):
                col_copy(d, k, j, lax.rem(my_col + cols - d, cols)).wait_recv()
                for e in range(1, rep):
                    rep_copy(e, d, k, j, my_rep).start()

    for j in range(each):
        send_rows(j)
        if j > 0:
            pass_cols(j - 1)
        pass_rows(j)
    pass_cols(each - 1)
    for j in range(each):
        for k in range(hidden):
            for d in range(cols):
                for e in range(1, rep):
                    rep_copy(e, d, k, j, lax.rem(my_rep + rep - e, rep)).wait_recv()

    examples = allp.shape[0]
    for p in range(block_p):
        rows = allp[:, p, :]
        upper = rows.astype(jnp.bfloat16)
        wide[0:examples, p * SKETCH : (p + 1) * SKETCH] = upper
        wide[examples:, p * SKETCH : (p + 1) * SKETCH] = (rows - upper.astype(jnp.float32)).astype(jnp.bfloat16)
    for k in range(gram_parts):
        load_gram(k).wait()

    share = psum.shape[2]
    step = 256
    per = share // step

    def send_sum(k):
        return pltpu.make_async_remote_copy(
            src_ref=psum.at[k],
            dst_ref=final.at[k],
            send_sem=send4.at[k],
            recv_sem=recv4.at[k],
            device_id={"hidden": to(k)},
            device_id_type=MESH,
        )

    def gram_step(n, carry):
        k = n // per
        at = pl.multiple_of(lax.rem(n, per) * step, step)
        column = pl.multiple_of(to(k) * share + at, step)
        both = jnp.dot(wide[...], gram_buf[:, pl.ds(column, step)], preferred_element_type=jnp.float32)
        psum[k, :, pl.ds(at, step)] = both[:examples] + both[examples:]

        @pl.when(jnp.logical_and(lax.rem(n, per) == per - 1, k < hidden - 1))
        def _():
            send_sum(k).start()

        return carry

    lax.fori_loop(0, hidden * per, gram_step, 0)
    total = psum[hidden - 1]
    for k in range(hidden - 1):
        send_sum(k).wait_recv()
        total = total + final[k]
    out_ref[...] = total

    for j in range(each):
        for k in range(hidden - 1):
            part_copy(k, j).wait_send()
            rows_copy(k, j, me).wait_send()
        for k in range(hidden):
            for d in range(1, cols):
                col_copy(d, k, j, my_col).wait_send()
            for d in range(cols):
                for e in range(1, rep):
                    rep_copy(e, d, k, j, my_rep).wait_send()
    for k in range(hidden - 1):
        send_sum(k).wait_send()


def fused(dims, inputs, grads, in_signs, out_signs, in_rows, out_rows, inv_gram):
    hidden, cols, rep = dims
    tokens = inputs.shape[0] // hidden
    count = inputs.shape[0] // SEQ
    each = count // hidden
    block_p = SKETCH // hidden
    examples = count * cols * rep
    share = inv_gram.shape[1] // hidden
    f32 = jnp.float32
    dma = pltpu.SemaphoreType.DMA
    vmem = pl.BlockSpec(memory_space=pltpu.VMEM)
    hbm = pl.BlockSpec(memory_space=pl.ANY)
    gram_parts = 4
    return pl.pallas_call(
        functools.partial(fused_kernel, dims),
        out_shape=jax.ShapeDtypeStruct((examples, share), f32),
        in_specs=[hbm, hbm, vmem, vmem, vmem, vmem, hbm],
        out_specs=vmem,
        scratch_shapes=[
            pltpu.VMEM((hidden, tokens, inputs.shape[1]), jnp.bfloat16),
            pltpu.VMEM((hidden, tokens, grads.shape[1]), jnp.bfloat16),
            pltpu.VMEM(inv_gram.shape, jnp.bfloat16),
            pltpu.VMEM((inputs.shape[1], SKETCH), jnp.bfloat16),
            pltpu.VMEM((grads.shape[1], SKETCH), jnp.bfloat16),
            pltpu.VMEM((hidden, each, 2, SEQ, SKETCH), f32),
            pltpu.VMEM((hidden + 1, each, 2, SEQ, SKETCH), f32),
            pltpu.VMEM((each, SKETCH, SKETCH), f32),
            pltpu.VMEM((examples, block_p, SKETCH), f32),
            pltpu.VMEM((2 * examples, block_p * SKETCH), jnp.bfloat16),
            pltpu.VMEM((hidden, examples, share), f32),
            pltpu.VMEM((hidden - 1, examples, share), f32),
            dma((hidden,)),
            dma((hidden,)),
            dma((gram_parts,)),
            dma((hidden - 1, each)),
            dma((hidden + 1, each)),
            dma((hidden - 1, each)),
            dma((hidden - 1, each)),
            dma((max(cols - 1, 1), hidden, each)),
            dma((max(cols - 1, 1), hidden, each)),
            dma((max(rep - 1, 1), cols, hidden, each)),
            dma((max(rep - 1, 1), cols, hidden, each)),
            dma((hidden - 1,)),
            dma((hidden - 1,)),
        ],
        compiler_params=pltpu.CompilerParams(
            collective_id=0, has_side_effects=True, vmem_limit_bytes=63 << 20
        ),
    )(
        inputs,
        grads,
        in_signs.reshape(inputs.shape[1] // (IN_W // HAD), IN_W // HAD),
        out_signs.reshape(grads.shape[1] // (OUT_W // HAD), OUT_W // HAD),
        in_rows.reshape(1, SKETCH),
        out_rows.reshape(1, SKETCH),
        inv_gram,
    )


def plain_sketch(values, signs, rows, width, shard):
    inner = width // HAD
    local_high = values.shape[1] // inner
    high, low = rows // inner, rows % inner
    feature = jnp.arange(values.shape[1], dtype=jnp.int32)
    sources = shard * local_high + feature // inner
    sign = (1 - 2 * had_parity(high[None, :], sources[:, None])) * signs[:, None]
    hit = (feature % inner)[:, None] == low[None, :]
    matrix = jnp.where(hit, sign.astype(jnp.float32) / math.sqrt(HAD), 0.0)
    return jnp.dot(values, matrix.astype(jnp.bfloat16), preferred_element_type=jnp.float32)


def plain(inputs, grads, in_signs, out_signs, in_rows, out_rows, inv_gram):
    shard = lax.axis_index("hidden")
    out_part = plain_sketch(grads, out_signs, out_rows, OUT_W, shard)
    in_part = plain_sketch(inputs, in_signs, in_rows, IN_W, shard)
    block_p = inv_gram.shape[0] // SKETCH
    count = inputs.shape[0] // SEQ
    out_mine = lax.psum_scatter(out_part, "hidden", scatter_dimension=1, tiled=True)
    in_sketch = lax.psum(in_part, "hidden")
    projected = jnp.einsum(
        "esp,esq->epq",
        out_mine.reshape(count, SEQ, block_p),
        in_sketch.reshape(count, SEQ, SKETCH),
        precision=lax.Precision.HIGHEST,
    )
    projected = projected.reshape(count, block_p * SKETCH)
    partial_out = jnp.dot(
        lax.all_gather(projected, ("cols", "rep"), axis=0, tiled=True),
        inv_gram.astype(jnp.float32),
        precision=lax.Precision.HIGHEST,
        preferred_element_type=jnp.float32,
    )
    return lax.psum_scatter(partial_out, "hidden", scatter_dimension=1, tiled=True)


def solution(mesh):
    dims = tuple(mesh.shape[name] for name in ("hidden", "cols", "rep"))

    def on_device(inputs, *rest):
        if dims[0] == 4 and inputs.shape[0] % (dims[0] * SEQ) == 0:
            return fused(dims, inputs, *rest)
        return plain(inputs, *rest)

    return jax.shard_map(
        on_device,
        mesh=mesh,
        in_specs=(
            P(("groups", "cols", "rep"), "hidden"),
            P(("groups", "cols", "rep"), "hidden"),
            P("hidden"),
            P("hidden"),
            P(),
            P(),
            P("hidden", ("cols", "rep")),
        ),
        out_specs=P("groups", ("cols", "rep", "hidden")),
        check_vma=False,
    )
```

```python
import functools
import math

import jax
import jax.numpy as jnp
from jax import lax
from jax.experimental import pallas as pl
from jax.experimental.pallas import tpu as pltpu
from jax.sharding import PartitionSpec as P

IN_W = 28672
OUT_W = 8192
HAD = 64
SKETCH = 128
SEQ = 128
LANES = 128
MESH = pl.DeviceIdType.MESH


def had_parity(left, right):
    both = jnp.bitwise_and(left, right)
    for shift in (4, 2, 1):
        both = jnp.bitwise_xor(both, jnp.right_shift(both, shift))
    return jnp.bitwise_and(both, 1)


def split_rows(rows, inner):
    high = jnp.floor((rows.astype(jnp.float32) + 0.5) * (1.0 / inner)).astype(jnp.int32)
    return high, rows - high * inner


def build_matrix(rows_ref, sign_ref, out_ref, shard, width):
    inner = width // HAD
    local_high = out_ref.shape[0] // inner
    high, low = split_rows(rows_ref[...], inner)
    hit = lax.broadcasted_iota(jnp.int32, (inner, SKETCH), 0) == low
    onehot = jnp.where(hit, 1.0, 0.0)
    sign = sign_ref[...].astype(jnp.float32).astype(jnp.bfloat16)
    line = lax.broadcasted_iota(jnp.int32, (sign.shape[0], SKETCH), 0)
    lane = lax.broadcasted_iota(jnp.int32, (LANES, SKETCH), 0)
    picked = {}
    for h in range(local_high):
        first, offset = divmod(h * inner, LANES)
        at = offset + low
        if offset not in picked:
            pick = jnp.where(lane == jnp.bitwise_and(at, LANES - 1), 1.0, 0.0).astype(jnp.bfloat16)
            picked[offset] = jnp.dot(sign, pick, preferred_element_type=jnp.float32)
        own = line == first + jnp.right_shift(at, LANES.bit_length() - 1)
        coef = jnp.sum(jnp.where(own, picked[offset], 0.0), axis=0, keepdims=True)
        parity = had_parity(high, shard * local_high + h)
        coef = coef * (1 - 2 * parity).astype(jnp.float32) * (1.0 / math.sqrt(HAD))
        out_ref[h * inner : (h + 1) * inner, :] = (onehot * coef).astype(jnp.bfloat16)


def fused_kernel(
    dims,
    x_ref,
    g_ref,
    in_sign_ref,
    out_sign_ref,
    in_rows_ref,
    out_rows_ref,
    gram_ref,
    out_ref,
    x_buf,
    g_buf,
    gram_buf,
    mat_in,
    mat_out,
    part,
    land,
    proj,
    allp,
    wide,
    psum,
    final,
    x_sem,
    g_sem,
    gram_sem,
    send1,
    recv1,
    send2,
    recv2,
    send3,
    recv3,
    send5,
    recv5,
    send4,
    recv4,
):
    hidden, cols, rep = dims
    me = lax.axis_index("hidden")
    my_col = lax.axis_index("cols")
    my_rep = lax.axis_index("rep")
    tokens = x_buf.shape[1]
    each = tokens // SEQ
    block_p = SKETCH // hidden

    def to(k):
        return lax.rem(me + 1 + k, hidden)

    def source(k):
        return lax.rem(me + 2 * hidden - 1 - k, hidden)

    def target(s):
        outer = 1 - lax.rem((me + 1) // 2, 2)
        first = outer * (3 - s) + (1 - outer) * lax.rem(2 + 3 * s, 5)
        return first + (me // 2) * (3 - 2 * first)

    def load_x(k):
        row = pl.multiple_of(target(k) * tokens, tokens)
        return pltpu.make_async_copy(x_ref.at[pl.ds(row, tokens)], x_buf.at[k], x_sem.at[k])

    def load_g(k):
        row = pl.multiple_of(target(k) * tokens, tokens)
        return pltpu.make_async_copy(g_ref.at[pl.ds(row, tokens)], g_buf.at[k], g_sem.at[k])

    gram_parts = gram_sem.shape[0]
    gram_rows = gram_ref.shape[0] // gram_parts

    def load_gram(k):
        where = pl.ds(k * gram_rows, gram_rows)
        return pltpu.make_async_copy(gram_ref.at[where], gram_buf.at[where], gram_sem.at[k])

    for k in range(hidden):
        load_g(k).start()
        load_x(k).start()

    barrier = pltpu.get_barrier_semaphore()
    for k in range(hidden - 1):
        pl.semaphore_signal(barrier, inc=1, device_id={"hidden": to(k)}, device_id_type=MESH)
    for c in range(1, cols):
        pl.semaphore_signal(barrier, inc=1, device_id={"cols": lax.rem(my_col + c, cols)}, device_id_type=MESH)
    for r in range(1, rep):
        pl.semaphore_signal(barrier, inc=1, device_id={"rep": lax.rem(my_rep + r, rep)}, device_id_type=MESH)
    build_matrix(out_rows_ref, out_sign_ref, mat_out, me, OUT_W)
    build_matrix(in_rows_ref, in_sign_ref, mat_in, me, IN_W)
    pl.semaphore_wait(barrier, hidden + cols + rep - 3)

    edge = 1 - lax.rem((me + 1) // 2, 2)
    half = me // 2
    relay = hidden

    def part_copy(s, j):
        passed = edge * (1 - (s + hidden - 1) // hidden)
        slot = me + passed * (relay - me)
        dest = target(s)
        return pltpu.make_async_remote_copy(
            src_ref=part.at[s, j],
            dst_ref=land.at[slot, j],
            send_sem=send1.at[s, j],
            recv_sem=recv1.at[slot, j],
            device_id={"hidden": dest + passed * (1 + half - dest)},
            device_id_type=MESH,
        )

    def part_arrived(slot, j):
        return pltpu.make_async_remote_copy(
            src_ref=part.at[0, j],
            dst_ref=land.at[slot, j],
            send_sem=send1.at[0, j],
            recv_sem=recv1.at[slot, j],
            device_id={"hidden": to(0)},
            device_id_type=MESH,
        )

    def sketch_step(s, carry):
        load_g(s).wait()
        left = jnp.dot(g_buf[s], mat_out[...], preferred_element_type=jnp.float32)
        load_x(s).wait()
        right = jnp.dot(x_buf[s], mat_in[...], preferred_element_type=jnp.float32)
        for j in range(each):
            part[s, j, 0] = left[j * SEQ : (j + 1) * SEQ]
            part[s, j, 1] = right[j * SEQ : (j + 1) * SEQ]

        @pl.when(s < hidden - 2 + edge)
        def _():
            part_copy(s, 0).start()

        return carry

    lax.fori_loop(0, hidden, sketch_step, 0)
    for j in range(1, each):
        for s in range(hidden - 2):
            part_copy(s, j).start()

        @pl.when(edge == 1)
        def _():
            part_copy(hidden - 2, j).start()

    for k in range(gram_parts):
        load_gram(k).start()

    @pl.when(edge == 0)
    def _():
        for j in range(each):
            part_arrived(relay, j).wait_recv()
            part[hidden - 2, j] = part[hidden - 2, j] + land[relay, j]
            part_copy(hidden - 2, j).start()

    def project(j):
        part_arrived(edge, j).wait_recv()
        part_arrived(hidden - 1 - edge, j).wait_recv()
        part[hidden - 1, j] = part[hidden - 1, j] + land[edge, j] + land[hidden - 1 - edge, j]

        @pl.when(edge == 0)
        def _():
            part_arrived(hidden - 1 - me, j).wait_recv()
            part[hidden - 1, j] = part[hidden - 1, j] + land[hidden - 1 - me, j]

        proj[j] = lax.dot_general(
            part[hidden - 1, j, 0],
            part[hidden - 1, j, 1],
            (((0,), (0,)), ((), ())),
            precision=lax.Precision.HIGHEST,
            preferred_element_type=jnp.float32,
        )

    def place(col, r, z, j):
        return ((col * rep + r) * hidden + z) * each + j

    def rows_copy(k, j, z):
        return pltpu.make_async_remote_copy(
            src_ref=proj.at[j, pl.ds(pl.multiple_of(to(k) * block_p, block_p), block_p), :],
            dst_ref=allp.at[place(my_col, my_rep, z, j)],
            send_sem=send2.at[k, j],
            recv_sem=recv2.at[k, j],
            device_id={"hidden": to(k)},
            device_id_type=MESH,
        )

    def col_copy(d, k, j, col):
        block = allp.at[place(col, my_rep, source(k), j)]
        return pltpu.make_async_remote_copy(
            src_ref=block,
            dst_ref=block,
            send_sem=send3.at[d - 1, k, j],
            recv_sem=recv3.at[d - 1, k, j],
            device_id={"cols": lax.rem(my_col + d, cols)},
            device_id_type=MESH,
        )

    def rep_copy(e, d, k, j, r):
        block = allp.at[place(lax.rem(my_col + cols - d, cols), r, source(k), j)]
        return pltpu.make_async_remote_copy(
            src_ref=block,
            dst_ref=block,
            send_sem=send5.at[e - 1, d, k, j],
            recv_sem=recv5.at[e - 1, d, k, j],
            device_id={"rep": lax.rem(my_rep + e, rep)},
            device_id_type=MESH,
        )

    def spread(k, j):
        for d in range(1, cols):
            col_copy(d, k, j, my_col).start()
        for e in range(1, rep):
            rep_copy(e, 0, k, j, my_rep).start()

    def send_rows(j):
        project(j)
        for k in range(hidden - 1):
            rows_copy(k, j, me).start()
        allp[place(my_col, my_rep, me, j)] = proj[j, pl.ds(pl.multiple_of(me * block_p, block_p), block_p), :]
        spread(hidden - 1, j)

    def pass_rows(j):
        for k in range(hidden - 1):
            rows_copy(k, j, source(k)).wait_recv()
            spread(k, j)

    def pass_cols(j):
        for d in range(1, cols):
            for k in [hidden - 1] + list(range(hidden - 1)):
                col_copy(d, k, j, lax.rem(my_col + cols - d, cols)).wait_recv()
                for e in range(1, rep):
                    rep_copy(e, d, k, j, my_rep).start()

    for j in range(each):
        send_rows(j)
        if j > 0:
            pass_cols(j - 1)
        pass_rows(j)
    pass_cols(each - 1)
    for j in range(each):
        for k in range(hidden):
            for d in range(cols):
                for e in range(1, rep):
                    rep_copy(e, d, k, j, lax.rem(my_rep + rep - e, rep)).wait_recv()

    examples = allp.shape[0]
    for p in range(block_p):
        rows = allp[:, p, :]
        upper = rows.astype(jnp.bfloat16)
        wide[0:examples, p * SKETCH : (p + 1) * SKETCH] = upper
        wide[examples:, p * SKETCH : (p + 1) * SKETCH] = (rows - upper.astype(jnp.float32)).astype(jnp.bfloat16)
    for k in range(gram_parts):
        load_gram(k).wait()

    per, step = psum.shape[1], psum.shape[3]

    def sum_copy(s, c):
        passed = edge * (1 - (s + hidden - 1) // hidden)
        slot = me + passed * (relay - me)
        dest = target(s)
        return pltpu.make_async_remote_copy(
            src_ref=psum.at[s, c],
            dst_ref=final.at[slot, c],
            send_sem=send4.at[s, c],
            recv_sem=recv4.at[slot, c],
            device_id={"hidden": dest + passed * (1 + half - dest)},
            device_id_type=MESH,
        )

    def sum_arrived(slot, c):
        return pltpu.make_async_remote_copy(
            src_ref=psum.at[0, c],
            dst_ref=final.at[slot, c],
            send_sem=send4.at[0, c],
            recv_sem=recv4.at[slot, c],
            device_id={"hidden": to(0)},
            device_id_type=MESH,
        )

    def gram_step(n, carry):
        s = n // per
        c = lax.rem(n, per)
        column = pl.multiple_of((target(s) * per + c) * step, step)
        both = jnp.dot(wide[...], gram_buf[:, pl.ds(column, step)], preferred_element_type=jnp.float32)
        psum[s, c] = both[:examples] + both[examples:]

        @pl.when(s < hidden - 2 + edge)
        def _():
            sum_copy(s, c).start()

        return carry

    lax.fori_loop(0, hidden * per, gram_step, 0)

    @pl.when(edge == 0)
    def _():
        for c in range(per):
            sum_arrived(relay, c).wait_recv()
            psum[hidden - 2, c] = psum[hidden - 2, c] + final[relay, c]
            sum_copy(hidden - 2, c).start()
        for c in range(per):
            sum_arrived(hidden - 1 - me, c).wait_recv()
            psum[hidden - 1, c] = psum[hidden - 1, c] + final[hidden - 1 - me, c]

    for c in range(per):
        sum_arrived(edge, c).wait_recv()
        sum_arrived(hidden - 1 - edge, c).wait_recv()
        out_ref[:, c * step : (c + 1) * step] = psum[hidden - 1, c] + final[edge, c] + final[hidden - 1 - edge, c]

    for j in range(each):
        for k in range(hidden - 1):
            part_copy(k, j).wait_send()
            rows_copy(k, j, me).wait_send()
        for k in range(hidden):
            for d in range(1, cols):
                col_copy(d, k, j, my_col).wait_send()
            for d in range(cols):
                for e in range(1, rep):
                    rep_copy(e, d, k, j, my_rep).wait_send()
    for k in range(hidden - 1):
        for c in range(per):
            sum_copy(k, c).wait_send()


def fused(dims, inputs, grads, in_signs, out_signs, in_rows, out_rows, inv_gram):
    hidden, cols, rep = dims
    tokens = inputs.shape[0] // hidden
    count = inputs.shape[0] // SEQ
    each = count // hidden
    block_p = SKETCH // hidden
    examples = count * cols * rep
    share = inv_gram.shape[1] // hidden
    per = share // 256
    f32 = jnp.float32
    dma = pltpu.SemaphoreType.DMA
    vmem = pl.BlockSpec(memory_space=pltpu.VMEM)
    hbm = pl.BlockSpec(memory_space=pl.ANY)
    gram_parts = 4
    return pl.pallas_call(
        functools.partial(fused_kernel, dims),
        out_shape=jax.ShapeDtypeStruct((examples, share), f32),
        in_specs=[hbm, hbm, vmem, vmem, vmem, vmem, hbm],
        out_specs=vmem,
        scratch_shapes=[
            pltpu.VMEM((hidden, tokens, inputs.shape[1]), jnp.bfloat16),
            pltpu.VMEM((hidden, tokens, grads.shape[1]), jnp.bfloat16),
            pltpu.VMEM(inv_gram.shape, jnp.bfloat16),
            pltpu.VMEM((inputs.shape[1], SKETCH), jnp.bfloat16),
            pltpu.VMEM((grads.shape[1], SKETCH), jnp.bfloat16),
            pltpu.VMEM((hidden, each, 2, SEQ, SKETCH), f32),
            pltpu.VMEM((hidden + 1, each, 2, SEQ, SKETCH), f32),
            pltpu.VMEM((each, SKETCH, SKETCH), f32),
            pltpu.VMEM((examples, block_p, SKETCH), f32),
            pltpu.VMEM((2 * examples, block_p * SKETCH), jnp.bfloat16),
            pltpu.VMEM((hidden, per, examples, share // per), f32),
            pltpu.VMEM((hidden + 1, per, examples, share // per), f32),
            dma((hidden,)),
            dma((hidden,)),
            dma((gram_parts,)),
            dma((hidden - 1, each)),
            dma((hidden + 1, each)),
            dma((hidden - 1, each)),
            dma((hidden - 1, each)),
            dma((max(cols - 1, 1), hidden, each)),
            dma((max(cols - 1, 1), hidden, each)),
            dma((max(rep - 1, 1), cols, hidden, each)),
            dma((max(rep - 1, 1), cols, hidden, each)),
            dma((hidden - 1, per)),
            dma((hidden + 1, per)),
        ],
        compiler_params=pltpu.CompilerParams(
            collective_id=0, has_side_effects=True, vmem_limit_bytes=63 << 20
        ),
    )(
        inputs,
        grads,
        in_signs.reshape(inputs.shape[1] // LANES, LANES),
        out_signs.reshape(grads.shape[1] // LANES, LANES),
        in_rows.reshape(1, SKETCH),
        out_rows.reshape(1, SKETCH),
        inv_gram,
    )


def plain_sketch(values, signs, rows, width, shard):
    inner = width // HAD
    local_high = values.shape[1] // inner
    high, low = rows // inner, rows % inner
    feature = jnp.arange(values.shape[1], dtype=jnp.int32)
    sources = shard * local_high + feature // inner
    sign = (1 - 2 * had_parity(high[None, :], sources[:, None])) * signs[:, None]
    hit = (feature % inner)[:, None] == low[None, :]
    matrix = jnp.where(hit, sign.astype(jnp.float32) / math.sqrt(HAD), 0.0)
    return jnp.dot(values, matrix.astype(jnp.bfloat16), preferred_element_type=jnp.float32)


def plain(inputs, grads, in_signs, out_signs, in_rows, out_rows, inv_gram):
    shard = lax.axis_index("hidden")
    out_part = plain_sketch(grads, out_signs, out_rows, OUT_W, shard)
    in_part = plain_sketch(inputs, in_signs, in_rows, IN_W, shard)
    block_p = inv_gram.shape[0] // SKETCH
    count = inputs.shape[0] // SEQ
    out_mine = lax.psum_scatter(out_part, "hidden", scatter_dimension=1, tiled=True)
    in_sketch = lax.psum(in_part, "hidden")
    projected = jnp.einsum(
        "esp,esq->epq",
        out_mine.reshape(count, SEQ, block_p),
        in_sketch.reshape(count, SEQ, SKETCH),
        precision=lax.Precision.HIGHEST,
    )
    projected = projected.reshape(count, block_p * SKETCH)
    partial_out = jnp.dot(
        lax.all_gather(projected, ("cols", "rep"), axis=0, tiled=True),
        inv_gram.astype(jnp.float32),
        precision=lax.Precision.HIGHEST,
        preferred_element_type=jnp.float32,
    )
    return lax.psum_scatter(partial_out, "hidden", scatter_dimension=1, tiled=True)


def solution(mesh):
    dims = tuple(mesh.shape[name] for name in ("hidden", "cols", "rep"))

    def on_device(inputs, *rest):
        if dims[0] == 4 and inputs.shape[0] % (dims[0] * SEQ) == 0:
            return fused(dims, inputs, *rest)
        return plain(inputs, *rest)

    return jax.shard_map(
        on_device,
        mesh=mesh,
        in_specs=(
            P(("groups", "cols", "rep"), "hidden"),
            P(("groups", "cols", "rep"), "hidden"),
            P("hidden"),
            P("hidden"),
            P(),
            P(),
            P("hidden", ("cols", "rep")),
        ),
        out_specs=P("groups", ("cols", "rep", "hidden")),
        check_vma=False,
    )
```

```python
import functools
import math

import jax
import jax.numpy as jnp
from jax import lax
from jax.experimental import pallas as pl
from jax.experimental.pallas import tpu as pltpu
from jax.sharding import PartitionSpec as P

IN_W = 28672
OUT_W = 8192
HAD = 64
SKETCH = 128
SEQ = 128
LANES = 128
MESH = pl.DeviceIdType.MESH


def had_parity(left, right):
    both = jnp.bitwise_and(left, right)
    for shift in (4, 2, 1):
        both = jnp.bitwise_xor(both, jnp.right_shift(both, shift))
    return jnp.bitwise_and(both, 1)


def split_rows(rows, inner):
    high = jnp.floor((rows.astype(jnp.float32) + 0.5) * (1.0 / inner)).astype(jnp.int32)
    return high, rows - high * inner


def build_matrix(rows_ref, sign_ref, out_ref, shard, width):
    inner = width // HAD
    local_high = out_ref.shape[0] // inner
    high, low = split_rows(rows_ref[...], inner)
    hit = lax.broadcasted_iota(jnp.int32, (inner, SKETCH), 0) == low
    onehot = jnp.where(hit, 1.0, 0.0)
    sign = sign_ref[...].astype(jnp.float32).astype(jnp.bfloat16)
    line = lax.broadcasted_iota(jnp.int32, (sign.shape[0], SKETCH), 0)
    lane = lax.broadcasted_iota(jnp.int32, (LANES, SKETCH), 0)
    picked = {}
    for h in range(local_high):
        first, offset = divmod(h * inner, LANES)
        at = offset + low
        if offset not in picked:
            pick = jnp.where(lane == jnp.bitwise_and(at, LANES - 1), 1.0, 0.0).astype(jnp.bfloat16)
            picked[offset] = jnp.dot(sign, pick, preferred_element_type=jnp.float32)
        own = line == first + jnp.right_shift(at, LANES.bit_length() - 1)
        coef = jnp.sum(jnp.where(own, picked[offset], 0.0), axis=0, keepdims=True)
        parity = had_parity(high, shard * local_high + h)
        coef = coef * (1 - 2 * parity).astype(jnp.float32) * (1.0 / math.sqrt(HAD))
        out_ref[h * inner : (h + 1) * inner, :] = (onehot * coef).astype(jnp.bfloat16)


def fused_kernel(
    dims,
    x_ref,
    g_ref,
    in_sign_ref,
    out_sign_ref,
    in_rows_ref,
    out_rows_ref,
    gram_ref,
    out_ref,
    x_buf,
    g_buf,
    gram_buf,
    mat_in,
    mat_out,
    part,
    land,
    proj,
    allp,
    wide,
    psum,
    final,
    x_sem,
    g_sem,
    gram_sem,
    send1,
    recv1,
    send2,
    recv2,
    send3,
    recv3,
    send5,
    recv5,
    send4,
    recv4,
):
    hidden, cols, rep = dims
    me = lax.axis_index("hidden")
    my_col = lax.axis_index("cols")
    my_rep = lax.axis_index("rep")
    tokens = x_buf.shape[1]
    each = tokens // SEQ
    block_p = SKETCH // hidden

    def to(k):
        return lax.rem(me + 1 + k, hidden)

    def source(k):
        return lax.rem(me + 2 * hidden - 1 - k, hidden)

    def target(s):
        outer = 1 - lax.rem((me + 1) // 2, 2)
        first = outer * (3 - s) + (1 - outer) * lax.rem(2 + 3 * s, 5)
        return first + (me // 2) * (3 - 2 * first)

    def load_x(k):
        row = pl.multiple_of(target(k) * tokens, tokens)
        return pltpu.make_async_copy(x_ref.at[pl.ds(row, tokens)], x_buf.at[k], x_sem.at[k])

    def load_g(k):
        row = pl.multiple_of(target(k) * tokens, tokens)
        return pltpu.make_async_copy(g_ref.at[pl.ds(row, tokens)], g_buf.at[k], g_sem.at[k])

    gram_parts = gram_sem.shape[0]
    gram_rows = gram_ref.shape[0] // gram_parts

    def load_gram(k):
        where = pl.ds(k * gram_rows, gram_rows)
        return pltpu.make_async_copy(gram_ref.at[where], gram_buf.at[where], gram_sem.at[k])

    for k in range(hidden):
        load_g(k).start()
        load_x(k).start()

    barrier = pltpu.get_barrier_semaphore()
    for k in range(hidden - 1):
        pl.semaphore_signal(barrier, inc=1, device_id={"hidden": to(k)}, device_id_type=MESH)
    for c in range(1, cols):
        pl.semaphore_signal(barrier, inc=1, device_id={"cols": lax.rem(my_col + c, cols)}, device_id_type=MESH)
    for r in range(1, rep):
        pl.semaphore_signal(barrier, inc=1, device_id={"rep": lax.rem(my_rep + r, rep)}, device_id_type=MESH)
    build_matrix(out_rows_ref, out_sign_ref, mat_out, me, OUT_W)
    build_matrix(in_rows_ref, in_sign_ref, mat_in, me, IN_W)
    pl.semaphore_wait(barrier, hidden + cols + rep - 3)

    edge = 1 - lax.rem((me + 1) // 2, 2)
    half = me // 2
    relay = hidden

    def part_copy(s, j):
        passed = edge * (1 - (s + hidden - 1) // hidden)
        slot = me + passed * (relay - me)
        dest = target(s)
        return pltpu.make_async_remote_copy(
            src_ref=part.at[s, j],
            dst_ref=land.at[slot, j],
            send_sem=send1.at[s, j],
            recv_sem=recv1.at[slot, j],
            device_id={"hidden": dest + passed * (1 + half - dest)},
            device_id_type=MESH,
        )

    def part_arrived(slot, j):
        return pltpu.make_async_remote_copy(
            src_ref=part.at[0, j],
            dst_ref=land.at[slot, j],
            send_sem=send1.at[0, j],
            recv_sem=recv1.at[slot, j],
            device_id={"hidden": to(0)},
            device_id_type=MESH,
        )

    def sketch_step(s, carry):
        load_g(s).wait()
        left = jnp.dot(g_buf[s], mat_out[...], preferred_element_type=jnp.float32)
        load_x(s).wait()
        right = jnp.dot(x_buf[s], mat_in[...], preferred_element_type=jnp.float32)
        for j in range(each):
            part[s, j, 0] = left[j * SEQ : (j + 1) * SEQ]
            part[s, j, 1] = right[j * SEQ : (j + 1) * SEQ]

        @pl.when(s < hidden - 2 + edge)
        def _():
            part_copy(s, 0).start()

        return carry

    lax.fori_loop(0, hidden, sketch_step, 0)
    for j in range(1, each):
        for s in range(hidden - 2):
            part_copy(s, j).start()

        @pl.when(edge == 1)
        def _():
            part_copy(hidden - 2, j).start()

    for k in range(gram_parts):
        load_gram(k).start()

    @pl.when(edge == 0)
    def _():
        for j in range(each):
            part_arrived(relay, j).wait_recv()
            part[hidden - 2, j] = part[hidden - 2, j] + land[relay, j]
            part_copy(hidden - 2, j).start()

    def project(j):
        part_arrived(edge, j).wait_recv()
        part_arrived(hidden - 1 - edge, j).wait_recv()
        part[hidden - 1, j] = part[hidden - 1, j] + land[edge, j] + land[hidden - 1 - edge, j]

        @pl.when(edge == 0)
        def _():
            part_arrived(hidden - 1 - me, j).wait_recv()
            part[hidden - 1, j] = part[hidden - 1, j] + land[hidden - 1 - me, j]

        proj[j] = lax.dot_general(
            part[hidden - 1, j, 0],
            part[hidden - 1, j, 1],
            (((0,), (0,)), ((), ())),
            precision=lax.Precision.HIGHEST,
            preferred_element_type=jnp.float32,
        )

    def place(col, r, z, j):
        return ((col * rep + r) * hidden + z) * each + j

    def rows_copy(k, j, z):
        return pltpu.make_async_remote_copy(
            src_ref=proj.at[j, pl.ds(pl.multiple_of(to(k) * block_p, block_p), block_p), :],
            dst_ref=allp.at[place(my_col, my_rep, z, j)],
            send_sem=send2.at[k, j],
            recv_sem=recv2.at[k, j],
            device_id={"hidden": to(k)},
            device_id_type=MESH,
        )

    def col_copy(d, k, j, col):
        block = allp.at[place(col, my_rep, source(k), j)]
        return pltpu.make_async_remote_copy(
            src_ref=block,
            dst_ref=block,
            send_sem=send3.at[d - 1, k, j],
            recv_sem=recv3.at[d - 1, k, j],
            device_id={"cols": lax.rem(my_col + d, cols)},
            device_id_type=MESH,
        )

    def rep_copy(e, d, k, j, r):
        block = allp.at[place(lax.rem(my_col + cols - d, cols), r, source(k), j)]
        return pltpu.make_async_remote_copy(
            src_ref=block,
            dst_ref=block,
            send_sem=send5.at[e - 1, d, k, j],
            recv_sem=recv5.at[e - 1, d, k, j],
            device_id={"rep": lax.rem(my_rep + e, rep)},
            device_id_type=MESH,
        )

    def spread(k, j):
        for d in range(1, cols):
            col_copy(d, k, j, my_col).start()
        for e in range(1, rep):
            rep_copy(e, 0, k, j, my_rep).start()

    def send_rows(j):
        project(j)
        for k in range(hidden - 1):
            rows_copy(k, j, me).start()
        allp[place(my_col, my_rep, me, j)] = proj[j, pl.ds(pl.multiple_of(me * block_p, block_p), block_p), :]
        spread(hidden - 1, j)

    def pass_rows(j):
        for k in range(hidden - 1):
            rows_copy(k, j, source(k)).wait_recv()
            spread(k, j)

    def pass_cols(j):
        for d in range(1, cols):
            for k in [hidden - 1] + list(range(hidden - 1)):
                col_copy(d, k, j, lax.rem(my_col + cols - d, cols)).wait_recv()
                for e in range(1, rep):
                    rep_copy(e, d, k, j, my_rep).start()

    for j in range(each):
        send_rows(j)
        if j > 0:
            pass_cols(j - 1)
        pass_rows(j)
    pass_cols(each - 1)
    for j in range(each):
        for k in range(hidden):
            for d in range(cols):
                for e in range(1, rep):
                    rep_copy(e, d, k, j, lax.rem(my_rep + rep - e, rep)).wait_recv()

    examples = allp.shape[0]
    for p in range(block_p):
        rows = allp[:, p, :]
        upper = rows.astype(jnp.bfloat16)
        wide[0:examples, p * SKETCH : (p + 1) * SKETCH] = upper
        wide[examples:, p * SKETCH : (p + 1) * SKETCH] = (rows - upper.astype(jnp.float32)).astype(jnp.bfloat16)
    for k in range(gram_parts):
        load_gram(k).wait()

    per, step = psum.shape[1], psum.shape[3]

    def sum_copy(s, c):
        passed = edge * (1 - (s + hidden - 1) // hidden)
        slot = me + passed * (relay - me)
        dest = target(s)
        return pltpu.make_async_remote_copy(
            src_ref=psum.at[s, c],
            dst_ref=final.at[slot, c],
            send_sem=send4.at[s, c],
            recv_sem=recv4.at[slot, c],
            device_id={"hidden": dest + passed * (1 + half - dest)},
            device_id_type=MESH,
        )

    def sum_arrived(slot, c):
        return pltpu.make_async_remote_copy(
            src_ref=psum.at[0, c],
            dst_ref=final.at[slot, c],
            send_sem=send4.at[0, c],
            recv_sem=recv4.at[slot, c],
            device_id={"hidden": to(0)},
            device_id_type=MESH,
        )

    def gram_step(n, carry):
        s = n // per
        c = lax.rem(n, per)
        column = pl.multiple_of((target(s) * per + c) * step, step)
        both = jnp.dot(wide[...], gram_buf[:, pl.ds(column, step)], preferred_element_type=jnp.float32)
        psum[s, c] = both[:examples] + both[examples:]

        @pl.when(s < hidden - 2 + edge)
        def _():
            sum_copy(s, c).start()

        return carry

    lax.fori_loop(0, hidden * per, gram_step, 0)

    @pl.when(edge == 0)
    def _():
        for c in range(per):
            sum_arrived(relay, c).wait_recv()
            psum[hidden - 2, c] = psum[hidden - 2, c] + final[relay, c]
            sum_copy(hidden - 2, c).start()
        for c in range(per):
            sum_arrived(hidden - 1 - me, c).wait_recv()
            psum[hidden - 1, c] = psum[hidden - 1, c] + final[hidden - 1 - me, c]

    for c in range(per):
        sum_arrived(edge, c).wait_recv()
        sum_arrived(hidden - 1 - edge, c).wait_recv()
        at = pl.ds(c * step, step)
        out_ref[0, :, at] = psum[hidden - 1, c] + final[edge, c]
        out_ref[1, :, at] = final[hidden - 1 - edge, c]

    for j in range(each):
        for k in range(hidden - 1):
            part_copy(k, j).wait_send()
            rows_copy(k, j, me).wait_send()
        for k in range(hidden):
            for d in range(1, cols):
                col_copy(d, k, j, my_col).wait_send()
            for d in range(cols):
                for e in range(1, rep):
                    rep_copy(e, d, k, j, my_rep).wait_send()
    for k in range(hidden - 1):
        for c in range(per):
            sum_copy(k, c).wait_send()


def fused(dims, inputs, grads, in_signs, out_signs, in_rows, out_rows, inv_gram):
    hidden, cols, rep = dims
    tokens = inputs.shape[0] // hidden
    count = inputs.shape[0] // SEQ
    each = count // hidden
    block_p = SKETCH // hidden
    examples = count * cols * rep
    share = inv_gram.shape[1] // hidden
    per = share // 256
    f32 = jnp.float32
    dma = pltpu.SemaphoreType.DMA
    vmem = pl.BlockSpec(memory_space=pltpu.VMEM)
    hbm = pl.BlockSpec(memory_space=pl.ANY)
    gram_parts = 4
    terms = pl.pallas_call(
        functools.partial(fused_kernel, dims),
        out_shape=jax.ShapeDtypeStruct((2, examples, share), f32),
        in_specs=[hbm, hbm, vmem, vmem, vmem, vmem, hbm],
        out_specs=vmem,
        scratch_shapes=[
            pltpu.VMEM((hidden, tokens, inputs.shape[1]), jnp.bfloat16),
            pltpu.VMEM((hidden, tokens, grads.shape[1]), jnp.bfloat16),
            pltpu.VMEM(inv_gram.shape, jnp.bfloat16),
            pltpu.VMEM((inputs.shape[1], SKETCH), jnp.bfloat16),
            pltpu.VMEM((grads.shape[1], SKETCH), jnp.bfloat16),
            pltpu.VMEM((hidden, each, 2, SEQ, SKETCH), f32),
            pltpu.VMEM((hidden + 1, each, 2, SEQ, SKETCH), f32),
            pltpu.VMEM((each, SKETCH, SKETCH), f32),
            pltpu.VMEM((examples, block_p, SKETCH), f32),
            pltpu.VMEM((2 * examples, block_p * SKETCH), jnp.bfloat16),
            pltpu.VMEM((hidden, per, examples, share // per), f32),
            pltpu.VMEM((hidden + 1, per, examples, share // per), f32),
            dma((hidden,)),
            dma((hidden,)),
            dma((gram_parts,)),
            dma((hidden - 1, each)),
            dma((hidden + 1, each)),
            dma((hidden - 1, each)),
            dma((hidden - 1, each)),
            dma((max(cols - 1, 1), hidden, each)),
            dma((max(cols - 1, 1), hidden, each)),
            dma((max(rep - 1, 1), cols, hidden, each)),
            dma((max(rep - 1, 1), cols, hidden, each)),
            dma((hidden - 1, per)),
            dma((hidden + 1, per)),
        ],
        compiler_params=pltpu.CompilerParams(
            collective_id=0, has_side_effects=True, vmem_limit_bytes=63 << 20
        ),
    )(
        inputs,
        grads,
        in_signs.reshape(inputs.shape[1] // LANES, LANES),
        out_signs.reshape(grads.shape[1] // LANES, LANES),
        in_rows.reshape(1, SKETCH),
        out_rows.reshape(1, SKETCH),
        inv_gram,
    )
    return terms[0] + terms[1]


def plain_sketch(values, signs, rows, width, shard):
    inner = width // HAD
    local_high = values.shape[1] // inner
    high, low = rows // inner, rows % inner
    feature = jnp.arange(values.shape[1], dtype=jnp.int32)
    sources = shard * local_high + feature // inner
    sign = (1 - 2 * had_parity(high[None, :], sources[:, None])) * signs[:, None]
    hit = (feature % inner)[:, None] == low[None, :]
    matrix = jnp.where(hit, sign.astype(jnp.float32) / math.sqrt(HAD), 0.0)
    return jnp.dot(values, matrix.astype(jnp.bfloat16), preferred_element_type=jnp.float32)


def plain(inputs, grads, in_signs, out_signs, in_rows, out_rows, inv_gram):
    shard = lax.axis_index("hidden")
    out_part = plain_sketch(grads, out_signs, out_rows, OUT_W, shard)
    in_part = plain_sketch(inputs, in_signs, in_rows, IN_W, shard)
    block_p = inv_gram.shape[0] // SKETCH
    count = inputs.shape[0] // SEQ
    out_mine = lax.psum_scatter(out_part, "hidden", scatter_dimension=1, tiled=True)
    in_sketch = lax.psum(in_part, "hidden")
    projected = jnp.einsum(
        "esp,esq->epq",
        out_mine.reshape(count, SEQ, block_p),
        in_sketch.reshape(count, SEQ, SKETCH),
        precision=lax.Precision.HIGHEST,
    )
    projected = projected.reshape(count, block_p * SKETCH)
    partial_out = jnp.dot(
        lax.all_gather(projected, ("cols", "rep"), axis=0, tiled=True),
        inv_gram.astype(jnp.float32),
        precision=lax.Precision.HIGHEST,
        preferred_element_type=jnp.float32,
    )
    return lax.psum_scatter(partial_out, "hidden", scatter_dimension=1, tiled=True)


def solution(mesh):
    dims = tuple(mesh.shape[name] for name in ("hidden", "cols", "rep"))

    def on_device(inputs, *rest):
        if dims[0] == 4 and inputs.shape[0] % (dims[0] * SEQ) == 0:
            return fused(dims, inputs, *rest)
        return plain(inputs, *rest)

    return jax.shard_map(
        on_device,
        mesh=mesh,
        in_specs=(
            P(("groups", "cols", "rep"), "hidden"),
            P(("groups", "cols", "rep"), "hidden"),
            P("hidden"),
            P("hidden"),
            P(),
            P(),
            P("hidden", ("cols", "rep")),
        ),
        out_specs=P("groups", ("cols", "rep", "hidden")),
        check_vma=False,
    )
```
